1024 devices in a mesh: seq: 16 (over y, x_hi), section: 16 (over z), mp: 4 (over x_lo, core).
Axes of the slice: x: 4 (x_hi: 2, x_lo: 2; x = x_hi * 2 + x_lo), y: 8, z: 16, core: 2. Of those that a mesh axis runs over, the one named last changes fastest.
Arguments:
- enc_rows: bfloat16 [16, 4096, 512], P('section', 'seq'), may hold values from -6 to 6
- proj_weight: bfloat16 [512, 8192], P(None, 'mp'), may hold values from -0.25 to 0.25
- row_owner: int32 [16, 4096], P('section', 'seq'), may hold values from -1 to 15, as said below
- grad_in: bfloat16 [16, 4096, 8192], P('section', 'seq', 'mp'), may hold values from -3 to 3
- adapter_gain: float32 [16, 8192], P('section', 'mp'), may hold values from 0.25 to 1.75
- adapter_down: bfloat16 [16, 64, 8192], P('section', None, 'mp'), may hold values from -0.375 to 0.375
- adapter_up: bfloat16 [16, 64, 8192], P('section', None, 'mp'), may hold values from -0.0625 to 0.0625
Outputs:
- soft_tokens: bfloat16 [16, 4096, 8192], P('section', 'seq', 'mp')
- enc_grad: float32 [16, 4096, 512], P('section', 'seq', 'mp')
The draws below stay inside these ranges and needn't reach their ends.
Inputs may be any that keep to these rules, and one draw needn't show every extreme that they name: row_owner[s, r] is the reader device along seq of encoder row r of micro-batch s, or -1 for an empty row. Every reader receives 16 to 256 rows of a micro-batch, and one reader exactly 256. One encoder device holds at most 16 rows for one reader, and exactly 16 for that fullest reader.
All inputs are finite; a program needn't handle non-finite values.
Results may differ from the reference program's by a relative error of at most 0.0061.
Values may be sent and summed in bfloat16 or wider, within the bound.
No kernel may reach another device: no remote copies, remote signals or barrier semaphores. Data moves between devices by JAX's collectives and lax.ppermute only.
A program may use at most 32 MiB of HBM per device.

```python
import jax
import jax.numpy as jnp
from jax import lax

D = 8192
G = 512
R = 64
SLOTS = 256
TICKS = 2
SECTIONS = 16
CAP = 16
ROWS = 4096
N_SEQ = 16
N_SECTION = 16


def owner_block(key):
    subkeys = jax.random.split(key, 5)
    extra_span = SLOTS - 16
    factor_one = jax.random.randint(subkeys[0], (N_SEQ,), 0, extra_span + 1)
    factor_two = jax.random.randint(subkeys[1], (N_SEQ,), 0, extra_span + 1)
    reader_loads = 16 + factor_one * factor_two // extra_span
    fullest = jax.random.randint(subkeys[2], (), 0, N_SEQ)
    readers = jnp.arange(N_SEQ, dtype=jnp.int32)
    reader_loads = jnp.where(readers == fullest, SLOTS, reader_loads).astype(jnp.int32)
    reader_order = jax.random.permutation(subkeys[3], N_SEQ).astype(jnp.int32)
    ordered = reader_loads[reader_order]
    run_ends = jnp.cumsum(ordered)
    position = jnp.arange(N_SEQ * SLOTS, dtype=jnp.int32)
    run_index = jnp.sum((position[:, None] >= run_ends[None, :]).astype(jnp.int32), axis=1)
    owners = jnp.where(run_index < N_SEQ, reader_order[jnp.minimum(run_index, N_SEQ - 1)], -1)
    layout = owners.reshape(SLOTS, N_SEQ).T
    shuffles = jax.vmap(lambda subkey: jax.random.permutation(subkey, SLOTS))(jax.random.split(subkeys[4], N_SEQ))
    layout = jnp.take_along_axis(layout, shuffles, axis=1)
    return layout.reshape(N_SEQ * SLOTS).astype(jnp.int32)


def draw_row_owner(key, part):
    return jax.vmap(owner_block)(jax.random.split(key, N_SECTION))


def level_of(key, shape, shards, low, top_value):
    loudness, own = 1.0, jax.random.fold_in(key, 6)
    for axis_at, parts in shards:
        draws = jnp.exp(jax.random.uniform(jax.random.fold_in(own, axis_at), (parts,), jnp.float32, low / len(shards), top_value / len(shards)))
        loudness = loudness * jnp.repeat(draws, shape[axis_at] // parts).reshape([-1 if axis == axis_at else 1 for axis in range(len(shape))])
    return loudness


def bell_draw(key, shape, scale, bound, cuts=(), kind=jnp.bfloat16):
    entries = scale * jax.random.normal(key, shape, jnp.float32)
    if cuts:
        entries = entries * level_of(key, shape, cuts, -0.22, 0.18)
    return jnp.clip(entries, -bound, bound).astype(kind)


def setup_inputs(seed: int = 0) -> dict:
    streams_of = jax.random.split(jax.random.key(seed), 8)
    enc_rows = bell_draw(streams_of[0], (SECTIONS, ROWS, G), 1.0, 6.0, ((0, 16), (1, 16)))
    proj_weight = bell_draw(streams_of[1], (G, D), G ** -0.5, 0.25, ((1, 4),))
    row_owner = draw_row_owner(jax.random.fold_in(streams_of[7], 71), 0)
    grad_in = bell_draw(streams_of[3], (SECTIONS, ROWS, D), 0.5, 3.0, ((0, 16), (1, 16), (2, 4)))
    adapter_gain = jnp.clip(1.0 + 0.15 * jax.random.normal(streams_of[4], (SECTIONS, D), jnp.float32), 0.25, 1.75)
    adapter_down = bell_draw(streams_of[5], (SECTIONS, R, D), (4 * R) ** -0.5, 0.375, ((0, 16), (2, 4)))
    adapter_up = bell_draw(streams_of[6], (SECTIONS, R, D), D ** -0.5, 0.0625, ((0, 16), (2, 4)))
    return dict(enc_rows=enc_rows, proj_weight=proj_weight, row_owner=row_owner, grad_in=grad_in, adapter_gain=adapter_gain, adapter_down=adapter_down, adapter_up=adapter_up)


def route_block(owners):
    readers = jnp.arange(N_SEQ, dtype=jnp.int32)
    matches = (owners[:, None] == readers[None, :]).astype(jnp.int32)
    before = jnp.cumsum(matches, axis=0) - matches
    return jnp.sum(matches * before, axis=1).astype(jnp.int32)


def adapter_back(carried, gain_row, down_rows, up_rows):
    reduced = jnp.dot(carried, up_rows.T, preferred_element_type=jnp.float32).astype(jnp.bfloat16)
    spread = jnp.dot(reduced, down_rows, preferred_element_type=jnp.float32)
    return (carried.astype(jnp.float32) + gain_row[None, :] * spread).astype(jnp.bfloat16)


def reference(enc_rows, proj_weight, row_owner, grad_in, adapter_gain, adapter_down, adapter_up):
    def one_segment(home):
        owners = row_owner[home].reshape(N_SEQ, SLOTS)
        order_rank = jax.vmap(route_block)(owners)
        encoder = jnp.arange(N_SEQ, dtype=jnp.int32)[:, None]
        is_valid = owners >= 0
        flat_slot = jnp.where(is_valid, owners * SLOTS + encoder * CAP + order_rank, ROWS).reshape(ROWS).astype(jnp.int32)
        projected = jnp.dot(enc_rows[home], proj_weight, preferred_element_type=jnp.float32).astype(jnp.bfloat16)
        soft_block = jnp.zeros((ROWS, D), jnp.bfloat16).at[flat_slot].set(projected, mode="drop")
        carried = grad_in[(home + TICKS) % SECTIONS]
        for tick_index in range(TICKS + 1):
            layer_index = (home + TICKS - tick_index) % SECTIONS
            carried = adapter_back(carried, adapter_gain[layer_index], adapter_down[layer_index], adapter_up[layer_index])
        picked = jnp.take(carried, jnp.minimum(flat_slot, ROWS - 1), axis=0)
        picked = jnp.where(is_valid.reshape(ROWS)[:, None], picked, jnp.zeros_like(picked))
        row_grads = jnp.dot(picked, proj_weight.T, preferred_element_type=jnp.float32)
        return soft_block, row_grads

    soft_tokens, enc_grad = lax.map(one_segment, jnp.arange(SECTIONS, dtype=jnp.int32))
    return soft_tokens, enc_grad
```

```python
import jax
import jax.numpy as jnp
from jax import lax
from jax.sharding import PartitionSpec as P

BF16 = jnp.bfloat16
F32 = jnp.float32


def send_along(value, axis, steps):
    count = lax.axis_size(axis)
    return lax.ppermute(value, axis, [(i, (i + steps) % count) for i in range(count)])


def dot(a, b, contract_a, contract_b):
    return lax.dot_general(a, b, (((contract_a,), (contract_b,)), ((), ())), preferred_element_type=F32)


def slots_of_rows(owners, readers, per_peer):
    rows = owners.shape[1]
    reader = lax.broadcasted_iota(jnp.int32, (readers, rows), 0)
    is_owner = reader == owners
    matches = is_owner.astype(BF16)
    earlier = (
        lax.broadcasted_iota(jnp.int32, (rows, rows), 0) < lax.broadcasted_iota(jnp.int32, (rows, rows), 1)
    ).astype(BF16)
    before = dot(matches, earlier, 1, 0)
    rank = jnp.sum(jnp.where(is_owner, before, 0.0), axis=0, keepdims=True).astype(jnp.int32)
    return jnp.where(owners >= 0, owners * per_peer + rank, -1)


def on_device(enc_rows, proj_weight, row_owner, grad_in, adapter_gain, adapter_down, adapter_up):
    readers = lax.axis_size("seq")
    feature_parts = lax.axis_size("mp")
    enc_block, grad = enc_rows[0], grad_in[0]
    slots = grad.shape[0]
    per_peer = slots // readers
    graph_width = enc_block.shape[1]
    part = graph_width // feature_parts
    up = adapter_up[0]
    rank = up.shape[0]

    up_one = send_along(up, "section", 1)
    up_zero = send_along(up, "section", 2)

    down = (adapter_down[0].astype(F32) * adapter_gain).astype(BF16)
    low_part = dot(up, grad, 1, 1)
    through_part = dot(down, proj_weight, 1, 1).astype(BF16)
    first = jnp.concatenate([low_part.astype(BF16), through_part], axis=1)
    first = jnp.sum(lax.all_gather(first, "mp").astype(F32), axis=0).astype(BF16)
    low_two, through = first[:, :slots], first[:, slots:]
    through_zero = send_along(through, "section", 2)
    carried = (grad.astype(F32) + dot(low_two, down, 0, 0)).astype(BF16)

    low_one_part = dot(up_one, carried, 1, 1).astype(BF16)
    cross_part = dot(down, up_one, 1, 1).astype(BF16)
    from_one = send_along(jnp.concatenate([through_part, cross_part], axis=1), "section", 1)
    low_one = jnp.sum(lax.all_gather(low_one_part, "mp").astype(F32), axis=0).astype(BF16)
    through_one_part, cross_one_part = from_one[:, :graph_width], from_one[:, graph_width:]
    low_zero_part = (dot(carried, up_zero, 1, 1) + dot(low_one, cross_one_part, 0, 0)).astype(BF16)
    slot_grads = (
        dot(carried, proj_weight, 1, 1)
        + dot(low_one, through_one_part, 0, 0)
        + dot(low_zero_part, through_zero, 1, 0)
    ).astype(BF16)

    target = slots_of_rows(row_owner, readers, per_peer)
    place = (lax.broadcasted_iota(jnp.int32, (slots, slots), 0) == target).astype(BF16)
    enc_part = lax.dynamic_slice_in_dim(enc_block, lax.axis_index("mp") * part, part, axis=1)
    routed = dot(place, enc_part, 1, 0).astype(BF16)

    back_blocks = slot_grads.reshape(readers, per_peer, feature_parts, part).transpose(0, 2, 1, 3)
    out_blocks = jnp.broadcast_to(
        routed.reshape(readers, 1, per_peer, part), (readers, feature_parts, per_peer, part)
    )
    blocks = jnp.concatenate([back_blocks, out_blocks], axis=3).reshape(readers * feature_parts, per_peer, 2 * part)
    blocks = lax.all_to_all(blocks, ("seq", "mp"), split_axis=0, concat_axis=0, tiled=True)
    blocks = blocks.reshape(readers, feature_parts, per_peer, 2 * part)
    returned = jnp.sum(blocks[..., :part].astype(F32), axis=1).astype(BF16).reshape(slots, part)
    returned = send_along(returned, "section", -2)
    arrived = blocks[..., part:].transpose(0, 2, 1, 3).reshape(slots, graph_width)
    soft_block = dot(arrived, proj_weight, 1, 0).astype(BF16)
    row_grads = dot(place, returned, 0, 0)
    return soft_block[None], row_grads[None]


def solution(mesh):
    placed = (
        P("section", "seq", None),
        P(None, "mp"),
        P("section", "seq"),
        P("section", "seq", "mp"),
        P("section", "mp"),
        P("section", None, "mp"),
        P("section", None, "mp"),
    )
    return jax.shard_map(
        on_device,
        mesh=mesh,
        in_specs=placed,
        out_specs=(P("section", "seq", "mp"), P("section", "seq", "mp")),
        check_vma=False,
    )
```

```python
import functools

import jax
import jax.numpy as jnp
from jax import lax
from jax.experimental import pallas as pl
from jax.experimental.pallas import tpu as pltpu
from jax.sharding import PartitionSpec as P

BF16 = jnp.bfloat16
F32 = jnp.float32


def send_along(value, axis, steps):
    count = lax.axis_size(axis)
    return lax.ppermute(value, axis, [(i, (i + steps) % count) for i in range(count)])


def dot(a, b, contract_a, contract_b):
    return lax.dot_general(a, b, (((contract_a,), (contract_b,)), ((), ())), preferred_element_type=F32)


def call_kernel(body, outs, *args):
    return pl.pallas_call(
        body,
        out_shape=[jax.ShapeDtypeStruct(shape, kind) for shape, kind in outs],
        in_specs=[pl.BlockSpec(memory_space=pltpu.VMEM)] * len(args),
        out_specs=[pl.BlockSpec(memory_space=pltpu.VMEM)] * len(outs),
        compiler_params=pltpu.CompilerParams(vmem_limit_bytes=24 << 20),
    )(*args)


def slots_of_rows(owners, readers, per_peer):
    rows = owners.shape[1]
    reader = lax.broadcasted_iota(jnp.int32, (readers, rows), 0)
    is_owner = reader == owners
    matches = jnp.where(is_owner, 1.0, 0.0).astype(BF16)
    earlier = lax.broadcasted_iota(jnp.int32, (rows, rows), 0) < lax.broadcasted_iota(jnp.int32, (rows, rows), 1)
    before = dot(matches, jnp.where(earlier, 1.0, 0.0).astype(BF16), 1, 0)
    rank = jnp.sum(jnp.where(is_owner, before, 0.0), axis=0, keepdims=True).astype(jnp.int32)
    return jnp.where(owners >= 0, owners * per_peer + rank, -1)


def relay_kernel(gathered_ref, first_ref, up_one_ref, scaled_ref, onward_ref, through_ref, low_two_ref):
    slots = low_two_ref.shape[1]
    rank, features = up_one_ref.shape
    width = through_ref.shape[1]
    onward_ref[:, :features] = up_one_ref[...]
    onward_ref[:, features : features + width] = first_ref[:, slots:]
    cross = dot(scaled_ref[...], up_one_ref[...], 1, 1).astype(BF16)
    onward_ref[:, features + width :] = jnp.concatenate([cross, jnp.zeros_like(cross)], axis=1)
    total = jnp.sum(gathered_ref[...].astype(F32), axis=0)
    low_two_ref[...] = total[:, :slots].astype(BF16)
    through_ref[...] = total[:, slots:].astype(BF16)


def carry_kernel(readers, owner_ref, enc_ref, grad_ref, low_two_ref, scaled_ref, up_one_ref, weight_ref,
                 carried_ref, low_one_ref, direct_ref, target_ref, routed_ref):
    slots = grad_ref.shape[0]
    low_two = low_two_ref[...].astype(F32).T.astype(BF16)
    carried = (grad_ref[...].astype(F32) + dot(low_two, scaled_ref[...], 1, 0)).astype(BF16)
    carried_ref[...] = carried
    low_one_ref[...] = dot(up_one_ref[...], carried, 1, 1).astype(BF16)
    direct_ref[...] = dot(carried, weight_ref[...], 1, 1)
    target = slots_of_rows(owner_ref[...], readers, slots // readers)
    target_ref[...] = target
    is_place = lax.broadcasted_iota(jnp.int32, (slots, slots), 0) == target
    place = jnp.where(is_place, 1.0, 0.0).astype(BF16)
    part = routed_ref.shape[1]
    mine = pl.multiple_of(lax.axis_index("mp") * part, part)
    routed_ref[...] = dot(place, enc_ref[:, pl.ds(mine, part)], 1, 0).astype(BF16)


def finish_kernel(gathered_ref, onward_ref, through_zero_ref, carried_ref, direct_ref, routed_ref, blocks_ref):
    features = carried_ref.shape[1]
    width = direct_ref.shape[1]
    rank = onward_ref.shape[0]
    readers, parts, rows, part = blocks_ref.shape
    pair = rows // 3
    low_one = jnp.sum(gathered_ref[...].astype(F32), axis=0)
    cross = onward_ref[:, features + width :].astype(F32)[:, :rank].T.astype(BF16)
    low_zero = dot(onward_ref[:, :features], carried_ref[...], 1, 1) + dot(cross, low_one.astype(BF16), 1, 0)
    lows = jnp.concatenate([low_one, low_zero], axis=0).T.astype(BF16)
    throughs = jnp.concatenate([onward_ref[:, features : features + width], through_zero_ref[...]], axis=0)
    slot_grads = direct_ref[...] + dot(lows, throughs, 1, 0)
    routed = routed_ref[...].astype(F32).reshape(readers, 2 * pair, part)
    for i in range(parts):
        block = slot_grads[:, i * part : (i + 1) * part].reshape(readers, 2 * pair, part)
        half = routed[:, (i % 2) * pair : (i % 2 + 1) * pair]
        blocks_ref[:, i] = jnp.concatenate([block, half], axis=1).astype(BF16)


def on_device(enc_rows, proj_weight, row_owner, grad_in, adapter_gain, adapter_down, adapter_up):
    readers = lax.axis_size("seq")
    feature_parts = lax.axis_size("mp")
    enc_block, grad, up, down = enc_rows[0], grad_in[0], adapter_up[0], adapter_down[0]
    slots = grad.shape[0]
    rank, features = up.shape
    per_peer = slots // readers
    width = enc_block.shape[1]
    part = width // feature_parts
    pair = per_peer // 2

    up_one = send_along(up, "section", 1)
    scaled = (down.astype(F32) * adapter_gain).astype(BF16)
    first = jnp.concatenate([dot(up, grad, 1, 1).astype(BF16), dot(scaled, proj_weight, 1, 1).astype(BF16)], axis=1)
    gathered = lax.all_gather(first, "mp")
    onward, through, low_two = call_kernel(
        relay_kernel,
        [((rank, features + width + 2 * rank), BF16), ((rank, width), BF16), ((rank, slots), BF16)],
        gathered, first, up_one, scaled,
    )
    onward = send_along(onward, "section", 1)
    through_zero = send_along(through, "section", 2)
    carried, low_one, direct, target, routed = call_kernel(
        functools.partial(carry_kernel, readers),
        [((slots, features), BF16), ((rank, slots), BF16), ((slots, width), F32), ((1, slots), jnp.int32), ((slots, part), BF16)],
        row_owner, enc_block, grad, low_two, scaled, up_one, proj_weight,
    )
    gathered = lax.all_gather(low_one, "mp")
    (blocks,) = call_kernel(
        finish_kernel,
        [((readers, feature_parts, per_peer + pair, part), BF16)],
        gathered, onward, through_zero, carried, direct, routed,
    )
    blocks = blocks.reshape(readers * feature_parts, per_peer + pair, part)
    blocks = lax.all_to_all(blocks, ("seq", "mp"), split_axis=0, concat_axis=0, tiled=True)
    blocks = blocks.reshape(readers, feature_parts, per_peer + pair, part)
    returned = jnp.sum(blocks[:, :, :per_peer].astype(F32), axis=1).astype(BF16).reshape(slots, part)
    returned = send_along(returned, "section", -2)
    own_half = blocks[:, :, per_peer:]
    other_half = lax.ppermute(own_half, "mp", [(i, i ^ 1) for i in range(feature_parts)])
    is_even = lax.axis_index("mp") % 2 == 0
    arrived = jnp.stack(
        [jnp.where(is_even, own_half, other_half), jnp.where(is_even, other_half, own_half)], axis=1
    )
    arrived = arrived.transpose(0, 1, 3, 2, 4).reshape(slots, width)
    soft_block = dot(arrived, proj_weight, 1, 0).astype(BF16)
    place = (lax.broadcasted_iota(jnp.int32, (slots, slots), 0) == target).astype(BF16)
    row_grads = dot(place, returned, 0, 0)
    return soft_block[None], row_grads[None]


def solution(mesh):
    placed = (
        P("section", "seq", None),
        P(None, "mp"),
        P("section", "seq"),
        P("section", "seq", "mp"),
        P("section", "mp"),
        P("section", None, "mp"),
        P("section", None, "mp"),
    )
    return jax.shard_map(
        on_device,
        mesh=mesh,
        in_specs=placed,
        out_specs=(P("section", "seq", "mp"), P("section", "seq", "mp")),
        check_vma=False,
    )
```

```python
import functools

import jax
import jax.numpy as jnp
from jax import lax
from jax.experimental import pallas as pl
from jax.experimental.pallas import tpu as pltpu
from jax.sharding import PartitionSpec as P

BF16 = jnp.bfloat16
F32 = jnp.float32


def send_along(value, axis, steps):
    count = lax.axis_size(axis)
    return lax.ppermute(value, axis, [(i, (i + steps) % count) for i in range(count)])


def dot(a, b, contract_a, contract_b):
    return lax.dot_general(a, b, (((contract_a,), (contract_b,)), ((), ())), preferred_element_type=F32)


def call_kernel(body, outs, *args):
    return pl.pallas_call(
        body,
        out_shape=[jax.ShapeDtypeStruct(shape, kind) for shape, kind in outs],
        in_specs=[pl.BlockSpec(memory_space=pltpu.VMEM)] * len(args),
        out_specs=[pl.BlockSpec(memory_space=pltpu.VMEM)] * len(outs),
        compiler_params=pltpu.CompilerParams(vmem_limit_bytes=24 << 20),
    )(*args)


def slots_of_rows(owners, readers, per_peer):
    rows = owners.shape[1]
    reader = lax.broadcasted_iota(jnp.int32, (readers, rows), 0)
    is_owner = reader == owners
    matches = jnp.where(is_owner, 1.0, 0.0).astype(BF16)
    earlier = lax.broadcasted_iota(jnp.int32, (rows, rows), 0) < lax.broadcasted_iota(jnp.int32, (rows, rows), 1)
    before = dot(matches, jnp.where(earlier, 1.0, 0.0).astype(BF16), 1, 0)
    rank = jnp.sum(jnp.where(is_owner, before, 0.0), axis=0, keepdims=True).astype(jnp.int32)
    return jnp.where(owners >= 0, owners * per_peer + rank, -1)


def scaled_down(down_ref, gain_ref):
    return (down_ref[...].astype(F32) * gain_ref[...]).astype(BF16)


def relay_kernel(gathered_ref, first_ref, up_one_ref, down_ref, gain_ref, onward_ref, through_ref, low_two_ref):
    slots = low_two_ref.shape[1]
    rank, features = up_one_ref.shape
    width = through_ref.shape[1]
    onward_ref[:, :features] = up_one_ref[...]
    onward_ref[:, features : features + width] = first_ref[:, slots:]
    cross = dot(scaled_down(down_ref, gain_ref), up_one_ref[...], 1, 1).astype(BF16)
    onward_ref[:, features + width :] = jnp.concatenate([cross, jnp.zeros_like(cross)], axis=1)
    total = jnp.sum(gathered_ref[...].astype(F32), axis=0)
    low_two_ref[...] = total[:, :slots].astype(BF16)
    through_ref[...] = total[:, slots:].astype(BF16)


def carry_kernel(readers, owner_ref, enc_ref, grad_ref, low_two_ref, down_ref, gain_ref, up_one_ref, weight_ref,
                 carried_ref, low_one_ref, direct_ref, target_ref, routed_ref):
    slots = grad_ref.shape[0]
    low_two = low_two_ref[...].astype(F32).T.astype(BF16)
    carried = (grad_ref[...].astype(F32) + dot(low_two, scaled_down(down_ref, gain_ref), 1, 0)).astype(BF16)
    carried_ref[...] = carried
    low_one_ref[...] = dot(up_one_ref[...], carried, 1, 1).astype(BF16)
    direct_ref[...] = dot(carried, weight_ref[...], 1, 1)
    target = slots_of_rows(owner_ref[...], readers, slots // readers)
    target_ref[...] = target
    is_place = lax.broadcasted_iota(jnp.int32, (slots, slots), 0) == target
    place = jnp.where(is_place, 1.0, 0.0).astype(BF16)
    part = routed_ref.shape[1]
    mine = pl.multiple_of(lax.axis_index("mp") * part, part)
    routed_ref[...] = dot(place, enc_ref[:, pl.ds(mine, part)], 1, 0).astype(BF16)


def finish_kernel(gathered_ref, onward_ref, through_zero_ref, carried_ref, direct_ref, routed_ref, blocks_ref):
    features = carried_ref.shape[1]
    width = direct_ref.shape[1]
    rank = onward_ref.shape[0]
    readers, parts, rows, part = blocks_ref.shape
    pair = rows // 3
    low_one = jnp.sum(gathered_ref[...].astype(F32), axis=0)
    cross = onward_ref[:, features + width :].astype(F32)[:, :rank].T.astype(BF16)
    low_zero = dot(onward_ref[:, :features], carried_ref[...], 1, 1) + dot(cross, low_one.astype(BF16), 1, 0)
    lows = jnp.concatenate([low_one, low_zero], axis=0).T.astype(BF16)
    throughs = jnp.concatenate([onward_ref[:, features : features + width], through_zero_ref[...]], axis=0)
    slot_grads = direct_ref[...] + dot(lows, throughs, 1, 0)
    routed = routed_ref[...].astype(F32).reshape(readers, 2 * pair, part)
    for i in range(parts):
        block = slot_grads[:, i * part : (i + 1) * part].reshape(readers, 2 * pair, part)
        half = routed[:, (i % 2) * pair : (i % 2 + 1) * pair]
        blocks_ref[:, i] = jnp.concatenate([block, half], axis=1).astype(BF16)


def pick_kernel(returned_ref, target_ref, grads_ref):
    slots = returned_ref.shape[0]
    is_place = lax.broadcasted_iota(jnp.int32, (slots, slots), 0) == target_ref[...]
    place = jnp.where(is_place, 1.0, 0.0).T.astype(BF16)
    grads_ref[...] = dot(place, returned_ref[...], 1, 0)


def soft_kernel(own_ref, other_ref, weight_ref, soft_hbm, soft_ref, written):
    pieces, slots, columns = soft_ref.shape
    parts = own_ref.shape[1]
    part = own_ref.shape[3]
    own = own_ref[...].astype(F32)
    other = other_ref[...].astype(F32)
    is_even = lax.axis_index("mp") % 2 == 0
    halves = jnp.concatenate([jnp.where(is_even, own, other), jnp.where(is_even, other, own)], axis=2)
    arrived = jnp.concatenate([halves[:, i].reshape(slots, part) for i in range(parts)], axis=1).astype(BF16)
    copies = []
    for j in range(pieces):
        soft_ref[j] = dot(arrived, weight_ref[:, j * columns : (j + 1) * columns], 1, 0).astype(BF16)
        copies.append(
            pltpu.make_async_copy(soft_ref.at[j], soft_hbm.at[:, pl.ds(j * columns, columns)], written.at[j])
        )
        copies[j].start()
    for copy in copies:
        copy.wait()


def call_soft(own, other, weight):
    readers, _, pair, _ = own.shape
    slots, features = readers * pair * 2, weight.shape[1]
    pieces = 4
    return pl.pallas_call(
        soft_kernel,
        out_shape=jax.ShapeDtypeStruct((slots, features), BF16),
        in_specs=[pl.BlockSpec(memory_space=pltpu.VMEM)] * 3,
        out_specs=pl.BlockSpec(memory_space=pl.ANY),
        scratch_shapes=[
            pltpu.VMEM((pieces, slots, features // pieces), BF16),
            pltpu.SemaphoreType.DMA((pieces,)),
        ],
        cost_estimate=pl.CostEstimate(flops=2 * slots * weight.size, transcendentals=0, bytes_accessed=2 * (slots * features + weight.size + 2 * own.size)),
        compiler_params=pltpu.CompilerParams(vmem_limit_bytes=24 << 20),
    )(own, other, weight)


def on_device(enc_rows, proj_weight, row_owner, grad_in, adapter_gain, adapter_down, adapter_up):
    readers = lax.axis_size("seq")
    feature_parts = lax.axis_size("mp")
    enc_block, grad, up, down = enc_rows[0], grad_in[0], adapter_up[0], adapter_down[0]
    slots = grad.shape[0]
    rank, features = up.shape
    per_peer = slots // readers
    width = enc_block.shape[1]
    part = width // feature_parts
    pair = per_peer // 2

    up_one = send_along(up, "section", 1)
    scaled = (down.astype(F32) * adapter_gain).astype(BF16)
    first = jnp.concatenate([dot(up, grad, 1, 1).astype(BF16), dot(scaled, proj_weight, 1, 1).astype(BF16)], axis=1)
    gathered = lax.all_gather(first, "mp")
    onward, through, low_two = call_kernel(
        relay_kernel,
        [((rank, features + width + 2 * rank), BF16), ((rank, width), BF16), ((rank, slots), BF16)],
        gathered, first, up_one, down, adapter_gain,
    )
    onward = send_along(onward, "section", 1)
    through_zero = send_along(through, "section", 2)
    carried, low_one, direct, target, routed = call_kernel(
        functools.partial(carry_kernel, readers),
        [((slots, features), BF16), ((rank, slots), BF16), ((slots, width), F32), ((1, slots), jnp.int32), ((slots, part), BF16)],
        row_owner, enc_block, grad, low_two, down, adapter_gain, up_one, proj_weight,
    )
    gathered = lax.all_gather(low_one, "mp")
    (blocks,) = call_kernel(
        finish_kernel,
        [((readers, feature_parts, per_peer + pair, part), BF16)],
        gathered, onward, through_zero, carried, direct, routed,
    )
    blocks = blocks.reshape(readers * feature_parts, per_peer + pair, part)
    blocks = lax.all_to_all(blocks, ("seq", "mp"), split_axis=0, concat_axis=0, tiled=True)
    blocks = blocks.reshape(readers, feature_parts, per_peer + pair, part)
    returned = jnp.sum(blocks[:, :, :per_peer].astype(F32), axis=1).astype(BF16).reshape(slots, part)
    returned = send_along(returned, "section", -2)
    own_half = blocks[:, :, per_peer:]
    other_half = lax.ppermute(own_half, "mp", [(i, i ^ 1) for i in range(feature_parts)])
    place = (lax.broadcasted_iota(jnp.int32, (slots, slots), 0) == target).astype(BF16)
    row_grads = dot(place, returned, 0, 0)
    soft_block = call_soft(own_half, other_half, proj_weight)
    return soft_block[None], row_grads[None]


def solution(mesh):
    placed = (
        P("section", "seq", None),
        P(None, "mp"),
        P("section", "seq"),
        P("section", "seq", "mp"),
        P("section", "mp"),
        P("section", None, "mp"),
        P("section", None, "mp"),
    )
    return jax.shard_map(
        on_device,
        mesh=mesh,
        in_specs=placed,
        out_specs=(P("section", "seq", "mp"), P("section", "seq", "mp")),
        check_vma=False,
    )
```
